1024 devices in a mesh: fsdp: 32 (over x, z_hi, core), expert: 32 (over z_lo, y).
Axes of the slice: x: 4, y: 8, z: 16 (z_hi: 4, z_lo: 4; z = z_hi * 4 + z_lo), core: 2. Of those that a mesh axis runs over, the one named last changes fastest.
Arguments:
- tokens: bfloat16 [256, 6144], P('expert', 'fsdp'), may hold values from -6 to 6
- cotangent: bfloat16 [256, 6144], P('expert', 'fsdp'), may hold values from -6 to 6
- routes: int32 [256, 2], P('expert'), may hold values from 0 to 3, all different within a row; in each aligned block of 8 rows (0 to 7, 8 to 15, ...) at most 8 rows name the same one
- route_weights: float32 [256, 2], P('expert'), may hold values from 0.1 to 0.9
- domains: int32 [256], P('expert'), may hold values from 0 to 7
- loss_weights: float32 [8], replicated, may hold values from 0.25 to 4
- w_gate: bfloat16 [32, 6144, 1536], P('expert', 'fsdp'), may hold values from -0.078125 to 0.078125
- w_up: bfloat16 [32, 6144, 1536], P('expert', 'fsdp'), may hold values from -0.078125 to 0.078125
- w_down: bfloat16 [32, 1536, 6144], P('expert', None, 'fsdp'), may hold values from -0.0546875 to 0.0546875
Outputs:
- mixed: bfloat16 [256, 6144], P('expert', 'fsdp')
- grad_tokens: bfloat16 [256, 6144], P('expert', 'fsdp')
- grad_gate: bfloat16 [32, 6144, 1536], P('expert', 'fsdp')
- grad_up: bfloat16 [32, 6144, 1536], P('expert', 'fsdp')
- grad_down: bfloat16 [32, 1536, 6144], P('expert', None, 'fsdp')
The draws below stay inside these ranges and needn't reach their ends.
Inputs may be any that keep to these rules, and one draw needn't show every extreme that they name: `routes`: each row names 2 different experts. Within the rows of one index of expert (aligned blocks of 8 rows) no expert is named more than 8 times, and in every draw some block names some expert exactly 8 times.
All inputs are finite; a program needn't handle non-finite values.
Results may differ from the reference program's by a relative error of at most 0.014.
Values may be sent and summed in bfloat16 or wider, within the bound.
No kernel may reach another device: no remote copies, remote signals or barrier semaphores. Data moves between devices by JAX's collectives and lax.ppermute only.
A program may use at most 32 MiB of HBM per device.

```python
import math
import jax
import jax.numpy as jnp
import numpy as np

D = 6144
FF = 12288
EXPERTS = 4
TOP = 2
DOMAINS = 8
TOK_BLOCK = 8
CAP = 8
TOKENS = 256
FF_GRP = 1536
N_EXPERT = 32


def set_ends(values, own_key, least, high):
    index_at = [jax.random.randint(jax.random.fold_in(own_key, axis), (), 0, length) for axis, length in enumerate(values.shape)]
    widest = values.shape.index(max(values.shape))
    neighbour = index_at[:widest] + [(index_at[widest] + 1) % values.shape[widest]] + index_at[widest + 1:]
    return values.at[tuple(index_at)].set(least).at[tuple(neighbour)].set(high)


def shard_levels(key, shape, shards, least, high):
    level, own = 1.0, jax.random.fold_in(key, 6)
    for axis_at, parts in shards:
        heights = jnp.exp(jax.random.uniform(jax.random.fold_in(own, axis_at), (parts,), jnp.float32, least / len(shards), high / len(shards)))
        level = level * jnp.repeat(heights, shape[axis_at] // parts).reshape([-1 if axis == axis_at else 1 for axis in range(len(shape))])
    return level


def routed_block(key, own, number, rows, count, top, limit, lean):
    order = jax.random.permutation(key, count)
    crowded, common = load_shares(count, rows * top, limit, lean, True), load_shares(count, rows * top, limit, lean, False)
    places = jnp.arange(count)

    def named(sizes, turn):
        used = int((sizes > 0).sum())
        fixed = max(1, used // 4)
        moved = fixed + (places - fixed + turn * (used - fixed)) % max(1, count - fixed)
        return jnp.zeros((count,), jnp.int32).at[order[jnp.where(places < fixed, places, moved)]].set(jnp.asarray(sizes, jnp.int32))

    sizes = jnp.where(number % 4 == 0, named(crowded, number // 4), named(common, number - number // 4 - 1))
    mixed = jax.random.permutation(jax.random.fold_in(own, 3), count)
    donor, sink = mixed[0:count // 2 * 2:2], mixed[1:count // 2 * 2:2]
    margin = jnp.minimum(sizes[donor] - 1, limit - sizes[sink]) // 2
    margin = jnp.where((donor == order[0]) | (sink == order[0]) | (sizes[sink] == 0), 0, jnp.maximum(margin, 0))
    moved = jax.random.randint(jax.random.fold_in(own, 4), (count // 2,), 0, 1 << 20) % (margin + 1)
    sizes = sizes.at[donor].add(-moved).at[sink].add(moved)
    labels = jnp.searchsorted(jnp.cumsum(sizes), jnp.arange(rows * top), side="right").astype(jnp.int32)
    grid = labels.reshape(top, rows).T
    grid = grid[jax.random.permutation(jax.random.fold_in(own, 1), rows)]
    turn = jax.random.randint(jax.random.fold_in(own, 2), (rows, 1), 0, top)
    return jnp.take_along_axis(grid, (jnp.arange(top)[None, :] + turn) % top, axis=1)


def load_shares(number_of, total, reach, lean, full):
    portions = [(1 << 20) // math.isqrt(standing ** lean) + 1 for standing in range(1, number_of + 1)]
    largest = reach if full else min(reach, max(-(-total // number_of), total * portions[0] // sum(portions)))
    least = 1 if total - largest >= number_of - 1 else 0
    counts, spare = [largest] + [least] * (number_of - 1), total - largest - least * (number_of - 1)
    while spare > 0:
        movable = [i for i in range(1, number_of) if counts[i] < largest] or [i for i in range(1, number_of) if counts[i] < reach]
        whole, remaining = sum([portions[i] for i in movable]), spare
        for i in movable:
            more = min(reach - counts[i], max(1, remaining * portions[i] // whole), spare)
            counts[i] = counts[i] + more
            spare = spare - more
    return np.array(counts)


def normal_values(stream_key, extent, spread, limit, pieces=(), kind=jnp.bfloat16):
    entries = jax.random.normal(stream_key, extent, jnp.float32) * spread
    if len(pieces) > 0:
        entries = shard_levels(stream_key, extent, pieces, -0.22, 0.18) * entries
    return jnp.clip(entries, min=-limit, max=limit).astype(kind)


def setup_inputs(seed: int = 0) -> dict:
    seeds = jax.random.split(jax.random.key(seed), 10)
    tokens = normal_values(seeds[0], (TOKENS, D), 1.0, 6.0, ((0, 32), (1, 32)))
    cotangent = normal_values(seeds[1], (TOKENS, D), 1.0, 6.0, ((0, 32), (1, 32)))
    routes_keys = jax.random.split(jax.random.fold_in(seeds[2], 1), TOKENS // TOK_BLOCK)
    routes_turns = jax.random.permutation(jax.random.fold_in(seeds[2], 3), TOKENS // TOK_BLOCK)
    routes = jax.vmap(lambda own, number: routed_block(jax.random.fold_in(seeds[2], 2), own, number, TOK_BLOCK, EXPERTS, TOP, CAP, 2))(routes_keys, routes_turns).reshape((TOKENS, TOP))
    route_weights = jnp.clip(0.1 + 0.79999997 * jax.random.uniform(seeds[3], (TOKENS, TOP), jnp.float32) ** shard_levels(seeds[3], (TOKENS, TOP), ((0, 32),), -0.2, 0.2), 0.1, 0.9)
    domains = set_ends(jax.random.randint(seeds[4], (TOKENS,), 0, DOMAINS), jax.random.fold_in(seeds[4], 1), 0, DOMAINS - 1).astype(jnp.int32)
    loss_weights = jnp.clip(jnp.exp(jax.random.uniform(seeds[5], (DOMAINS,), jnp.float32, math.log(0.25), math.log(4.0))), 0.25, 4.0)
    w_gate = normal_values(seeds[6], (N_EXPERT, D, FF_GRP), D ** -0.5, 0.078125, ((0, 32), (1, 32)))
    w_up = normal_values(seeds[7], (N_EXPERT, D, FF_GRP), D ** -0.5, 0.078125, ((0, 32), (1, 32)))
    w_down = normal_values(seeds[8], (N_EXPERT, FF_GRP, D), FF ** -0.5, 0.0546875, ((0, 32), (2, 32)))
    return dict(tokens=tokens, cotangent=cotangent, routes=routes, route_weights=route_weights, domains=domains, loss_weights=loss_weights, w_gate=w_gate, w_up=w_up, w_down=w_down)


def reference(tokens, cotangent, routes, route_weights, domains, loss_weights, w_gate, w_up, w_down):
    groups = N_EXPERT // EXPERTS
    grp_width = FF // groups
    gate_full = w_gate.reshape(EXPERTS, groups, D, grp_width).transpose(0, 2, 1, 3).reshape(EXPERTS, D, FF)
    up_full = w_up.reshape(EXPERTS, groups, D, grp_width).transpose(0, 2, 1, 3).reshape(EXPERTS, D, FF)
    down_full = w_down.reshape(EXPERTS, FF, D)
    domain_hit = domains[:, None] == jnp.arange(DOMAINS, dtype=jnp.int32)[None, :]
    token_scale = jnp.sum(jnp.where(domain_hit, loss_weights[None, :], jnp.float32(0.0)), axis=1)
    scaled = (cotangent.astype(jnp.float32) * token_scale[:, None]).astype(jnp.bfloat16)
    most_rows = TOKENS
    mixed_acc = jnp.zeros((TOKENS, D), jnp.float32)
    grad_acc = jnp.zeros((TOKENS, D), jnp.float32)
    gate_grads = []
    up_grads = []
    down_grads = []
    for expert_id in range(EXPERTS):
        named = routes == expert_id
        chosen = jnp.any(named, axis=1)
        weight_row = jnp.sum(jnp.where(named, route_weights, jnp.float32(0.0)), axis=1)
        where_rows = jnp.nonzero(chosen, size=most_rows, fill_value=0)[0].astype(jnp.int32)
        valid = jnp.arange(most_rows, dtype=jnp.int32) < jnp.sum(chosen.astype(jnp.int32))
        row_weight = jnp.where(valid, weight_row[where_rows], jnp.float32(0.0))
        inputs = jnp.where(valid[:, None], tokens[where_rows], jnp.zeros((), jnp.bfloat16)).astype(jnp.bfloat16)
        gate = jnp.dot(inputs, gate_full[expert_id], preferred_element_type=jnp.float32)
        upper = jnp.dot(inputs, up_full[expert_id], preferred_element_type=jnp.float32)
        sigma = jax.nn.sigmoid(gate)
        hidden = (gate * sigma * upper).astype(jnp.bfloat16)
        expert_out = jnp.dot(hidden, down_full[expert_id], preferred_element_type=jnp.float32)
        mixed_acc = mixed_acc.at[where_rows].add(row_weight[:, None] * expert_out)
        out_grad = (row_weight[:, None] * scaled[where_rows].astype(jnp.float32)).astype(jnp.bfloat16)
        hidden_grad = jnp.dot(out_grad, down_full[expert_id].T, preferred_element_type=jnp.float32)
        gate_grad = (hidden_grad * upper * sigma * (1.0 + gate * (1.0 - sigma))).astype(jnp.bfloat16)
        up_grad = (hidden_grad * gate * sigma).astype(jnp.bfloat16)
        input_grad = jnp.dot(gate_grad, gate_full[expert_id].T, preferred_element_type=jnp.float32)
        input_grad = input_grad + jnp.dot(up_grad, up_full[expert_id].T, preferred_element_type=jnp.float32)
        grad_acc = grad_acc.at[where_rows].add(input_grad)
        gate_grads.append(jnp.dot(inputs.T, gate_grad, preferred_element_type=jnp.float32))
        up_grads.append(jnp.dot(inputs.T, up_grad, preferred_element_type=jnp.float32))
        down_grads.append(jnp.dot(hidden.T, out_grad, preferred_element_type=jnp.float32))
    grad_gate = jnp.stack(gate_grads).reshape(EXPERTS, D, groups, grp_width).transpose(0, 2, 1, 3)
    grad_gate = grad_gate.reshape(N_EXPERT, D, grp_width).astype(jnp.bfloat16)
    grad_up = jnp.stack(up_grads).reshape(EXPERTS, D, groups, grp_width).transpose(0, 2, 1, 3)
    grad_up = grad_up.reshape(N_EXPERT, D, grp_width).astype(jnp.bfloat16)
    grad_down = jnp.stack(down_grads).reshape(N_EXPERT, grp_width, D).astype(jnp.bfloat16)
    return (mixed_acc.astype(jnp.bfloat16), grad_acc.astype(jnp.bfloat16), grad_gate, grad_up, grad_down)
```

```python
import jax
import jax.numpy as jnp
from jax import lax
from jax.experimental import pallas as pl
from jax.sharding import Mesh, PartitionSpec as P

EXPERTS = 4
DOMAINS = 8
CHUNKS = 1
INTERPRET = False
F32 = jnp.float32
LOW = jnp.bfloat16
NN = (((1,), (0,)), ((), ()))
NT = (((1,), (1,)), ((), ()))
TN = (((0,), (0,)), ((), ()))


def mm(a, b, dims):
    return lax.dot_general(a, b, dims, preferred_element_type=F32)


def partial_kernel(x_ref, g_ref, wg_ref, wu_ref, wd_ref, out_ref):
    width = wg_ref.shape[2]
    x = x_ref[...]
    out_ref[:, :width] = mm(x, wg_ref[0], NN).astype(LOW)
    out_ref[:, width : 2 * width] = mm(x, wu_ref[0], NN).astype(LOW)
    out_ref[:, 2 * width :] = mm(g_ref[...], wd_ref[0], NN).astype(LOW)


def middle_kernel(parts_ref, out_ref):
    copies, _, columns = parts_ref.shape
    width = columns // 3
    total = parts_ref[0].astype(F32)
    for i in range(1, copies):
        total = total + parts_ref[i].astype(F32)
    gate = total[:, :width]
    up = total[:, width : 2 * width]
    hidden_grad = total[:, 2 * width :]
    sigma = jax.nn.sigmoid(gate)
    hidden = (gate * sigma * up).astype(LOW)
    gate_grad = (hidden_grad * up * sigma * (1.0 + gate * (1.0 - sigma))).astype(LOW)
    up_grad = (hidden_grad * gate * sigma).astype(LOW)
    for i in range(copies):
        out_ref[i, :, :width] = hidden
        out_ref[i, :, width : 2 * width] = gate_grad
        out_ref[i, :, 2 * width :] = up_grad


def rows_kernel(*refs):
    acts, (wg_ref, wu_ref, wd_ref, out_ref, in_ref) = refs[:-5], refs[-5:]
    out = None
    for i, act_ref in enumerate(acts):
        width = act_ref.shape[1] // 3
        cols = slice(i * width, (i + 1) * width)
        o = mm(act_ref[:, :width], wd_ref[0, :, cols], NT)
        g = mm(act_ref[:, width : 2 * width], wg_ref[0, :, cols], NT)
        g = g + mm(act_ref[:, 2 * width :], wu_ref[0, :, cols], NT)
        out, back = (o, g) if out is None else (out + o, back + g)
    out_ref[...] = out.astype(LOW)
    in_ref[...] = back.astype(LOW)


def grads_kernel(*refs):
    acts, (x_ref, g_ref, gg_ref, gu_ref, gd_ref) = refs[:-5], refs[-5:]
    for i, act_ref in enumerate(acts):
        width = act_ref.shape[1] // 3
        cols = slice(i * width, (i + 1) * width)
        gd_ref[0, :, cols] = mm(g_ref[...], act_ref[:, :width], TN).astype(LOW)
        gg_ref[0, :, cols] = mm(x_ref[...], act_ref[:, width : 2 * width], TN).astype(LOW)
        gu_ref[0, :, cols] = mm(x_ref[...], act_ref[:, 2 * width :], TN).astype(LOW)


def call(kernel, shapes, *args, **extra):
    return pl.pallas_call(kernel, out_shape=shapes, interpret=INTERPRET, **extra)(*args)


def exchange(value, axis):
    return lax.all_to_all(value, axis, split_axis=0, concat_axis=0, tiled=True)


def scatter_sum(value, axis, count):
    rows, columns = value.shape
    parts = exchange(value.reshape(count, rows // count, columns), axis)
    return jnp.sum(parts.astype(F32), axis=0).astype(LOW)


def gather_rows(value, axis, count):
    rows, columns = value.shape
    copies = jnp.broadcast_to(value[None], (count, rows, columns))
    return exchange(copies, axis).reshape(count * rows, columns)


def per_device(
    tokens, cotangent, routes, route_weights, domains, loss_weights, w_gate, w_up, w_down
):
    tok_count, local_width = tokens.shape
    n_x, n_z, n_core = lax.axis_size("x"), lax.axis_size("z_hi"), lax.axis_size("core")
    groups = lax.axis_size("y")
    owners = EXPERTS * groups
    rows = owners * tok_count
    grp_width = w_gate.shape[2]
    width = grp_width // CHUNKS
    w_down_t = jnp.swapaxes(w_down, 1, 2)

    named = routes[None, :, :] == jnp.arange(EXPERTS, dtype=jnp.int32)[:, None, None]
    chosen = jnp.any(named, axis=2)
    weight = jnp.sum(jnp.where(named, route_weights[None], F32(0.0)), axis=2)
    domain_hit = domains[:, None] == jnp.arange(DOMAINS, dtype=jnp.int32)[None, :]
    token_scale = jnp.sum(jnp.where(domain_hit, loss_weights[None, :], F32(0.0)), axis=1)
    scaled = (cotangent.astype(F32) * token_scale[:, None]).astype(LOW)
    send_x = jnp.where(chosen[:, :, None], tokens[None], jnp.zeros((), LOW))
    send_g = (weight[:, :, None] * scaled[None].astype(F32)).astype(LOW)
    send = jnp.stack([send_x, send_g], axis=1)
    send = jnp.broadcast_to(send[:, None], (EXPERTS, groups, 2, tok_count, local_width))
    got = exchange(send.reshape(owners, 2, tok_count, local_width), ("z_lo", "y"))
    x_rows = got[:, 0].reshape(rows, local_width)
    g_rows = got[:, 1].reshape(rows, local_width)

    acts = []
    for chunk in range(CHUNKS):
        whole = pl.BlockSpec((rows, local_width), lambda i: (0, 0))
        part = pl.BlockSpec((1, local_width, width), lambda i, chunk=chunk: (0, 0, chunk))
        sums = call(
            partial_kernel,
            jax.ShapeDtypeStruct((rows, 3 * width), LOW),
            x_rows,
            g_rows,
            w_gate,
            w_up,
            w_down_t,
            grid=(1,),
            in_specs=[whole, whole, part, part, part],
            out_specs=pl.BlockSpec((rows, 3 * width), lambda i: (0, 0)),
        )
        sums = scatter_sum(sums, "core", n_core)
        sums = scatter_sum(sums, "x", n_x)
        last = sums.shape[0] // n_z
        parts = exchange(sums.reshape(n_z, last, 3 * width), "z_hi")
        copies = call(middle_kernel, jax.ShapeDtypeStruct(parts.shape, LOW), parts)
        act = exchange(copies, "z_hi").reshape(n_z * last, 3 * width)
        act = gather_rows(act, "x", n_x)
        act = gather_rows(act, "core", n_core)
        acts.append(act)

    flat = jax.ShapeDtypeStruct((rows, local_width), LOW)
    out_part, in_part = call(rows_kernel, (flat, flat), *acts, w_gate, w_up, w_down_t)
    back = jnp.stack(
        [
            out_part.reshape(owners, tok_count, local_width),
            in_part.reshape(owners, tok_count, local_width),
        ],
        axis=1,
    )
    back = exchange(back, ("z_lo", "y"))
    grad = jax.ShapeDtypeStruct((1, local_width, grp_width), LOW)
    grad_gate, grad_up, grad_down = call(grads_kernel, (grad, grad, grad), *acts, x_rows, g_rows)
    back = back.reshape(EXPERTS, groups, 2, tok_count, local_width).astype(F32)
    mixed = jnp.sum(weight[:, :, None] * jnp.sum(back[:, :, 0], axis=1), axis=0)
    grad_tokens = jnp.sum(back[:, :, 1], axis=(0, 1))
    return (
        mixed.astype(LOW),
        grad_tokens.astype(LOW),
        grad_gate,
        grad_up,
        jnp.swapaxes(grad_down, 1, 2),
    )


def solution(mesh):
    n_fsdp, n_expert = mesh.shape["fsdp"], mesh.shape["expert"]
    n_x = 4 if n_fsdp >= 32 else 2
    split = (n_x, n_fsdp // (2 * n_x), 2, EXPERTS, n_expert // EXPERTS)
    fine = Mesh(mesh.devices.reshape(split), ("x", "z_hi", "core", "z_lo", "y"))
    fsdp, expert = ("x", "z_hi", "core"), ("z_lo", "y")
    in_specs = (
        P(expert, fsdp),
        P(expert, fsdp),
        P(expert, None),
        P(expert, None),
        P(expert),
        P(),
        P(expert, fsdp, None),
        P(expert, fsdp, None),
        P(expert, None, fsdp),
    )
    out_specs = (
        P(expert, fsdp),
        P(expert, fsdp),
        P(expert, fsdp, None),
        P(expert, fsdp, None),
        P(expert, None, fsdp),
    )
    return jax.shard_map(
        per_device, mesh=fine, in_specs=in_specs, out_specs=out_specs, check_vma=False
    )
```

```python
import jax
import jax.numpy as jnp
from jax import lax
from jax.experimental import pallas as pl
from jax.experimental.pallas import tpu as pltpu
from jax.sharding import Mesh, PartitionSpec as P

EXPERTS = 4
TOP = 2
BLOCK_COLS = 512
INTERPRET = False
F32 = jnp.float32
LOW = jnp.bfloat16
NN = (((1,), (0,)), ((), ()))
NT = (((1,), (1,)), ((), ()))
TN = (((0,), (0,)), ((), ()))


def mm(a, b, dims):
    return lax.dot_general(a, b, dims, preferred_element_type=F32)


def column(values):
    spots = lax.broadcasted_iota(jnp.int32, (len(values), 1), 0)
    out = jnp.zeros((len(values), 1), F32)
    for t, value in enumerate(values):
        out = jnp.where(spots == t, value, out)
    return out


def expert_column(routes_ref, values, expert, count):
    picked = []
    for t in range(count):
        total = F32(0.0)
        for k in range(TOP):
            total = total + jnp.where(routes_ref[k, t] == expert, values(k, t), F32(0.0))
        picked.append(total)
    return column(picked)


def send_kernel(routes_ref, weights_ref, domains_ref, loss_ref, tok_ref, cot_ref, out_ref):
    count = tok_ref.shape[0]
    groups = out_ref.shape[0] // EXPERTS
    scale = column([loss_ref[domains_ref[t]] for t in range(count)])
    scaled = (cot_ref[...].astype(F32) * scale).astype(LOW).astype(F32)
    tok = tok_ref[...].astype(F32)
    for expert in range(EXPERTS):
        weight = expert_column(routes_ref, lambda k, t: weights_ref[k, t], expert, count)
        named = expert_column(routes_ref, lambda k, t: F32(1.0), expert, count)
        x_part = jnp.where(named > 0.0, tok, F32(0.0)).astype(LOW)
        g_part = (weight * scaled).astype(LOW)
        for group in range(groups):
            out_ref[expert * groups + group, 0] = x_part
            out_ref[expert * groups + group, 1] = g_part


def final_kernel(routes_ref, weights_ref, back_ref, mixed_ref, grad_ref):
    count = back_ref.shape[2]
    groups = back_ref.shape[0] // EXPERTS
    mixed, grad = None, None
    for expert in range(EXPERTS):
        weight = expert_column(routes_ref, lambda k, t: weights_ref[k, t], expert, count)
        out = back_ref[expert * groups, 0].astype(F32)
        inner = back_ref[expert * groups, 1].astype(F32)
        for group in range(1, groups):
            out = out + back_ref[expert * groups + group, 0].astype(F32)
            inner = inner + back_ref[expert * groups + group, 1].astype(F32)
        out = weight * out
        mixed = out if mixed is None else mixed + out
        grad = inner if grad is None else grad + inner
    mixed_ref[...] = mixed.astype(LOW)
    grad_ref[...] = grad.astype(LOW)


def rows_of(ref, which):
    blocks, _, count, width = ref.shape
    return ref[:, which].reshape(blocks * count, width)


def partial_kernel(half_ref, got_ref, wg_ref, wu_ref, wd_ref, out_ref):
    width = wg_ref.shape[2]
    x = rows_of(got_ref, 0)
    out_ref[:, :width] = mm(x, wg_ref[0], NN).astype(LOW)
    out_ref[:, width : 2 * width] = mm(x, wu_ref[0], NN).astype(LOW)
    out_ref[:, 2 * width :] = mm(rows_of(got_ref, 1), wd_ref[0], NN).astype(LOW)


def middle_kernel(parts_ref, out_ref):
    copies, _, columns = parts_ref.shape
    for start in range(0, columns, 3 * BLOCK_COLS):
        cols = [
            slice(start + i * BLOCK_COLS, start + (i + 1) * BLOCK_COLS) for i in range(3)
        ]
        sums = []
        for col in cols:
            total = parts_ref[0, :, col].astype(F32)
            for i in range(1, copies):
                total = total + parts_ref[i, :, col].astype(F32)
            sums.append(total)
        gate, up, hidden_grad = sums
        sigma = jax.nn.sigmoid(gate)
        hidden = (gate * sigma * up).astype(LOW)
        gate_grad = (hidden_grad * up * sigma * (1.0 + gate * (1.0 - sigma))).astype(LOW)
        up_grad = (hidden_grad * gate * sigma).astype(LOW)
        for i in range(copies):
            for col, value in zip(cols, (hidden, gate_grad, up_grad)):
                out_ref[i, :, col] = value


def row_products(act_ref, wg_ref, wu_ref, wd_ref, out_acc, in_acc):
    width = wg_ref.shape[2]
    step = pl.program_id(0)

    @pl.when(step == 0)
    def _():
        out_acc[...] = jnp.zeros_like(out_acc)
        in_acc[...] = jnp.zeros_like(in_acc)

    out_acc[...] += mm(act_ref[:, :width], wd_ref[0], NT)
    inner = mm(act_ref[:, width : 2 * width], wg_ref[0], NT)
    in_acc[...] += inner + mm(act_ref[:, 2 * width :], wu_ref[0], NT)


def store_rows(back_ref, out_acc, in_acc):
    blocks, _, count, width = back_ref.shape

    @pl.when(pl.program_id(0) == pl.num_programs(0) - 1)
    def _():
        back_ref[:, 0] = out_acc[...].reshape(blocks, count, width).astype(LOW)
        back_ref[:, 1] = in_acc[...].reshape(blocks, count, width).astype(LOW)


def own_kernel(half_ref, act_ref, wg_ref, wu_ref, wd_ref, back_ref, out_acc, in_acc):
    row_products(act_ref, wg_ref, wu_ref, wd_ref, out_acc, in_acc)
    store_rows(back_ref, out_acc, in_acc)


def tail_kernel(
    half_ref,
    own_ref,
    other_ref,
    own_got_ref,
    other_got_ref,
    wg_ref,
    wu_ref,
    wd_ref,
    held_ref,
    back_ref,
    gg_ref,
    gu_ref,
    gd_ref,
    out_acc,
    in_acc,
):
    width = wg_ref.shape[2]
    row_products(other_ref, wg_ref, wu_ref, wd_ref, out_acc, in_acc)
    x = jnp.concatenate([rows_of(own_got_ref, 0), rows_of(other_got_ref, 0)], axis=0)
    g = jnp.concatenate([rows_of(own_got_ref, 1), rows_of(other_got_ref, 1)], axis=0)
    act = jnp.concatenate([own_ref[...], other_ref[...]], axis=0)
    gd_ref[0] = mm(g, act[:, :width], TN).astype(LOW)
    gg_ref[0] = mm(x, act[:, width : 2 * width], TN).astype(LOW)
    gu_ref[0] = mm(x, act[:, 2 * width :], TN).astype(LOW)
    store_rows(back_ref, out_acc, in_acc)


def exchange(value, axis):
    return lax.all_to_all(value, axis, split_axis=0, concat_axis=0, tiled=True)


def per_device(
    tokens, cotangent, routes, route_weights, domains, loss_weights, w_gate, w_up, w_down
):
    tok_count, local_width = tokens.shape
    n_x, n_z, n_core = lax.axis_size("x"), lax.axis_size("z_hi"), lax.axis_size("core")
    owners = EXPERTS * lax.axis_size("y")
    grp_width = w_gate.shape[2]
    steps = grp_width // BLOCK_COLS
    columns = 3 * grp_width
    half_rows = owners * tok_count // n_core
    w_down_t = jnp.swapaxes(w_down, 1, 2)
    routes_t = routes.T
    weights_t = route_weights.T
    half = lax.axis_index("core").reshape(1).astype(jnp.int32)
    swap = [(0, 1), (1, 0)]

    small = pl.BlockSpec(memory_space=pltpu.SMEM)
    plain = pl.BlockSpec(memory_space=pltpu.VMEM)
    flat = jax.ShapeDtypeStruct((tok_count, local_width), LOW)
    block = jax.ShapeDtypeStruct((owners, 2, tok_count, local_width), LOW)
    send = pl.pallas_call(
        send_kernel,
        out_shape=block,
        in_specs=[small, small, small, small, plain, plain],
        interpret=INTERPRET,
    )(routes_t, weights_t, domains, loss_weights, tokens, cotangent)
    send, half = lax.optimization_barrier((send, half))
    got = exchange(send, ("z_lo", "y"))

    def quarter(other):
        return pl.BlockSpec(
            (owners // n_core, 2, tok_count, local_width),
            lambda j, half_ref: (1 - half_ref[0] if other else half_ref[0], 0, 0, 0),
        )

    weight = pl.BlockSpec((1, local_width, BLOCK_COLS), lambda j, half_ref: (0, 0, j))
    act_spec = pl.BlockSpec((half_rows, 3 * BLOCK_COLS), lambda j, half_ref: (0, j))
    anywhere = pl.BlockSpec(memory_space=pl.ANY)
    accs = [pltpu.VMEM((half_rows, local_width), F32)] * 2

    def run(kernel, in_specs, out_specs, shapes, scratch, aliases, *args):
        return pl.pallas_call(
            kernel,
            out_shape=shapes,
            grid_spec=pltpu.PrefetchScalarGridSpec(
                num_scalar_prefetch=1,
                grid=(steps,),
                in_specs=in_specs,
                out_specs=out_specs,
                scratch_shapes=scratch,
            ),
            input_output_aliases=aliases,
            interpret=INTERPRET,
        )(half, *args)

    def partial(other):
        return run(
            partial_kernel,
            [quarter(other), weight, weight, weight],
            act_spec,
            jax.ShapeDtypeStruct((half_rows, columns), LOW),
            [],
            {},
            got,
            w_gate,
            w_up,
            w_down_t,
        )

    arrived = lax.ppermute(partial(True), "core", swap)
    sums = (partial(False).astype(F32) + arrived.astype(F32)).astype(LOW)
    parts = exchange(sums.reshape(n_x, half_rows // n_x, columns), "x")
    sums = jnp.sum(parts.astype(F32), axis=0).astype(LOW)
    parts = exchange(sums.reshape(n_z, sums.shape[0] // n_z, columns), "z_hi")
    copies = pl.pallas_call(
        middle_kernel, out_shape=jax.ShapeDtypeStruct(parts.shape, LOW), interpret=INTERPRET
    )(parts)
    act = exchange(copies, "z_hi").reshape(1, half_rows // n_x, columns)
    act = exchange(jnp.broadcast_to(act, (n_x,) + act.shape[1:]), "x")
    own = act.reshape(half_rows, columns)
    other = lax.ppermute(own, "core", swap)

    back = run(
        own_kernel,
        [act_spec, weight, weight, weight],
        quarter(False),
        block,
        accs,
        {},
        own,
        w_gate,
        w_up,
        w_down_t,
    )
    grad = jax.ShapeDtypeStruct((1, local_width, grp_width), LOW)
    back, grad_gate, grad_up, grad_down = run(
        tail_kernel,
        [act_spec, act_spec, quarter(False), quarter(True), weight, weight, weight, anywhere],
        [quarter(True), weight, weight, weight],
        (block, grad, grad, grad),
        accs,
        {8: 0},
        own,
        other,
        got,
        got,
        w_gate,
        w_up,
        w_down_t,
        back,
    )
    back = exchange(back, ("z_lo", "y"))
    mixed, grad_tokens = pl.pallas_call(
        final_kernel,
        out_shape=(flat, flat),
        in_specs=[small, small, plain],
        interpret=INTERPRET,
    )(routes_t, weights_t, back)
    return mixed, grad_tokens, grad_gate, grad_up, jnp.swapaxes(grad_down, 1, 2)


def solution(mesh):
    n_fsdp, n_expert = mesh.shape["fsdp"], mesh.shape["expert"]
    n_x = 4 if n_fsdp >= 32 else 2
    split = (n_x, n_fsdp // (2 * n_x), 2, EXPERTS, n_expert // EXPERTS)
    fine = Mesh(mesh.devices.reshape(split), ("x", "z_hi", "core", "z_lo", "y"))
    fsdp, expert = ("x", "z_hi", "core"), ("z_lo", "y")
    in_specs = (
        P(expert, fsdp),
        P(expert, fsdp),
        P(expert, None),
        P(expert, None),
        P(expert),
        P(),
        P(expert, fsdp, None),
        P(expert, fsdp, None),
        P(expert, None, fsdp),
    )
    out_specs = (
        P(expert, fsdp),
        P(expert, fsdp),
        P(expert, fsdp, None),
        P(expert, fsdp, None),
        P(expert, None, fsdp),
    )
    return jax.shard_map(
        per_device, mesh=fine, in_specs=in_specs, out_specs=out_specs, check_vma=False
    )
```

```python
import jax
import jax.numpy as jnp
from jax import lax
from jax.experimental import pallas as pl
from jax.experimental.pallas import tpu as pltpu
from jax.sharding import Mesh, PartitionSpec as P

EXPERTS = 4
TOP = 2
LIMIT = 8 * 2**20
TAIL_LIMIT = 16 * 2**20
INTERPRET = False
F32 = jnp.float32
LOW = jnp.bfloat16
NN = (((1,), (0,)), ((), ()))
NT = (((1,), (1,)), ((), ()))
TN = (((0,), (0,)), ((), ()))


def mm(a, b, dims):
    return lax.dot_general(a, b, dims, preferred_element_type=F32)


def column(values):
    spots = lax.broadcasted_iota(jnp.int32, (len(values), 1), 0)
    out = jnp.zeros((len(values), 1), F32)
    for t, value in enumerate(values):
        out = jnp.where(spots == t, value, out)
    return out


def expert_column(routes_ref, values, expert, count):
    picked = []
    for t in range(count):
        total = F32(0.0)
        for k in range(TOP):
            total = total + jnp.where(routes_ref[k, t] == expert, values(k, t), F32(0.0))
        picked.append(total)
    return column(picked)


def send_kernel(routes_ref, weights_ref, domains_ref, loss_ref, tok_ref, cot_ref, out_ref):
    count = tok_ref.shape[0]
    groups = out_ref.shape[0] // EXPERTS
    scale = column([loss_ref[domains_ref[t]] for t in range(count)])
    scaled = (cot_ref[...].astype(F32) * scale).astype(LOW).astype(F32)
    tok = tok_ref[...].astype(F32)
    for expert in range(EXPERTS):
        weight = expert_column(routes_ref, lambda k, t: weights_ref[k, t], expert, count)
        named = expert_column(routes_ref, lambda k, t: F32(1.0), expert, count)
        x_part = jnp.where(named > 0.0, tok, F32(0.0)).astype(LOW)
        g_part = (weight * scaled).astype(LOW)
        for group in range(groups):
            out_ref[expert * groups + group, 0] = x_part
            out_ref[expert * groups + group, 1] = g_part


def final_kernel(routes_ref, weights_ref, back_ref, mixed_ref, grad_ref):
    count = back_ref.shape[2]
    groups = back_ref.shape[0] // EXPERTS
    mixed, grad = None, None
    for expert in range(EXPERTS):
        weight = expert_column(routes_ref, lambda k, t: weights_ref[k, t], expert, count)
        out = back_ref[expert * groups, 0].astype(F32)
        inner = back_ref[expert * groups, 1].astype(F32)
        for group in range(1, groups):
            out = out + back_ref[expert * groups + group, 0].astype(F32)
            inner = inner + back_ref[expert * groups + group, 1].astype(F32)
        out = weight * out
        mixed = out if mixed is None else mixed + out
        grad = inner if grad is None else grad + inner
    mixed_ref[...] = mixed.astype(LOW)
    grad_ref[...] = grad.astype(LOW)


def rows_of(ref, half, which):
    blocks = ref.shape[0] // 2
    _, _, count, width = ref.shape
    return ref[pl.ds(half * blocks, blocks), which].reshape(blocks * count, width)


def partial_kernel(half_ref, got_ref, wg_ref, wu_ref, wd_ref, out_ref, bufs, sems):
    width = bufs.shape[2]
    half = half_ref[0]
    copies = []
    for i, weight_ref in enumerate((wg_ref, wu_ref, wd_ref)):
        copy = pltpu.make_async_copy(weight_ref.at[0], bufs.at[i], sems.at[i])
        copy.start()
        copies.append(copy)
    for i, copy in enumerate(copies):
        rows = rows_of(got_ref, half, 1 if i == 2 else 0)
        copy.wait()
        out_ref[:, i * width : (i + 1) * width] = mm(rows, bufs[i], NN).astype(LOW)


def middle_kernel(parts_ref, out_ref):
    copies, _, columns = parts_ref.shape
    width = columns // 3
    total = parts_ref[0].astype(F32)
    for i in range(1, copies):
        total = total + parts_ref[i].astype(F32)
    gate = total[:, :width]
    up = total[:, width : 2 * width]
    hidden_grad = total[:, 2 * width :]
    sigma = jax.nn.sigmoid(gate)
    hidden = (gate * sigma * up).astype(LOW)
    gate_grad = (hidden_grad * up * sigma * (1.0 + gate * (1.0 - sigma))).astype(LOW)
    up_grad = (hidden_grad * gate * sigma).astype(LOW)
    for i in range(copies):
        out_ref[i, :, :width] = hidden
        out_ref[i, :, width : 2 * width] = gate_grad
        out_ref[i, :, 2 * width :] = up_grad


def row_products(act_ref, wg_ref, wu_ref, wd_ref):
    width = wg_ref.shape[2]
    out = mm(act_ref[:, :width], wd_ref[0], NT)
    inner = mm(act_ref[:, width : 2 * width], wg_ref[0], NT)
    return out, inner + mm(act_ref[:, 2 * width :], wu_ref[0], NT)


def own_kernel(act_ref, wg_ref, wu_ref, wd_ref, back_ref):
    blocks, _, count, width = back_ref.shape
    out, inner = row_products(act_ref, wg_ref, wu_ref, wd_ref)
    back_ref[:, 0] = out.reshape(blocks, count, width).astype(LOW)
    back_ref[:, 1] = inner.reshape(blocks, count, width).astype(LOW)


def tail_kernel(
    half_ref,
    own_ref,
    other_ref,
    got_ref,
    held_ref,
    wg_ref,
    wu_ref,
    wd_ref,
    back_ref,
    gg_ref,
    gu_ref,
    gd_ref,
    gg_buf,
    gu_buf,
    gd_buf,
    sems,
):
    width = wg_ref.shape[2]
    blocks, _, count, rows_width = held_ref.shape
    half = half_ref[0]
    act = jnp.concatenate([own_ref[...], other_ref[...]], axis=0)
    copies = []
    for i, (which, buf, dst) in enumerate(
        ((1, gd_buf, gd_ref), (0, gg_buf, gg_ref), (0, gu_buf, gu_ref))
    ):
        rows = [rows_of(got_ref, half, which), rows_of(got_ref, 1 - half, which)]
        rows = jnp.concatenate(rows, axis=0)
        buf[0] = mm(rows, act[:, i * width : (i + 1) * width], TN).astype(LOW)
        copy = pltpu.make_async_copy(buf, dst, sems.at[i])
        copy.start()
        copies.append(copy)
    out, inner = row_products(other_ref, wg_ref, wu_ref, wd_ref)
    back_ref[pl.ds(half * blocks, blocks)] = held_ref[...]
    other = pl.ds((1 - half) * blocks, blocks)
    back_ref[other, 0] = out.reshape(blocks, count, rows_width).astype(LOW)
    back_ref[other, 1] = inner.reshape(blocks, count, rows_width).astype(LOW)
    for copy in copies:
        copy.wait()


def near(value):
    return value if INTERPRET else pltpu.with_memory_space_constraint(value, pltpu.VMEM)


def far(value):
    return value if INTERPRET else pltpu.with_memory_space_constraint(value, pltpu.HBM)


def near_out(shape):
    return jax.ShapeDtypeStruct(shape, LOW) if INTERPRET else pltpu.VMEM(shape, LOW)


def call(kernel, in_specs, out_specs, shapes, args, limit, scratch=()):
    return pl.pallas_call(
        kernel,
        out_shape=shapes,
        in_specs=in_specs,
        out_specs=out_specs,
        scratch_shapes=scratch,
        compiler_params=pltpu.CompilerParams(vmem_limit_bytes=limit),
        interpret=INTERPRET,
    )(*args)


def exchange(value, axis):
    return lax.all_to_all(value, axis, split_axis=0, concat_axis=0, tiled=True)


def per_device(
    tokens, cotangent, routes, route_weights, domains, loss_weights, w_gate, w_up, w_down
):
    tok_count, local_width = tokens.shape
    n_x, n_z, n_core = lax.axis_size("x"), lax.axis_size("z_hi"), lax.axis_size("core")
    owners = EXPERTS * lax.axis_size("y")
    grp_width = w_gate.shape[2]
    columns = 3 * grp_width
    half_rows = owners * tok_count // n_core
    routes_t = routes.T
    weights_t = route_weights.T
    half = lax.axis_index("core").reshape(1).astype(jnp.int32)
    swap = [(0, 1), (1, 0)]
    plain_weights = (w_gate, w_up, jnp.swapaxes(w_down, 1, 2))
    far_weights = [far(w) for w in plain_weights]
    weights = [near(w) for w in plain_weights]

    smem = pl.BlockSpec(memory_space=pltpu.SMEM)
    vmem = pl.BlockSpec(memory_space=pltpu.VMEM)
    hbm = pl.BlockSpec(memory_space=pl.ANY)
    block = (owners, 2, tok_count, local_width)
    send = call(
        send_kernel,
        [smem] * 4 + [vmem] * 2,
        vmem,
        jax.ShapeDtypeStruct(block, LOW),
        (routes_t, weights_t, domains, loss_weights, tokens, cotangent),
        None,
    )
    send, half, rest = lax.optimization_barrier((send, half, 1 - half))
    got = near(exchange(send, ("z_lo", "y")))

    def partial(which):
        return call(
            partial_kernel,
            [smem, vmem] + [pl.BlockSpec(memory_space=pl.ANY if INTERPRET else pltpu.HBM)] * 3,
            vmem,
            near_out((half_rows, columns)),
            (which, got, *far_weights),
            LIMIT,
            [
                pltpu.VMEM((3, local_width, grp_width), LOW),
                pltpu.SemaphoreType.DMA((3,)),
            ],
        )

    arrived = lax.ppermute(partial(rest), "core", swap)
    sums = (partial(half).astype(F32) + arrived.astype(F32)).astype(LOW)
    parts = exchange(sums.reshape(n_x, half_rows // n_x, columns), "x")
    sums = jnp.sum(parts.astype(F32), axis=0).astype(LOW)
    parts = exchange(sums.reshape(n_z, sums.shape[0] // n_z, columns), "z_hi")
    copies = call(middle_kernel, [vmem], vmem, near_out(parts.shape), (near(parts),), LIMIT)
    act = exchange(copies, "z_hi").reshape(1, half_rows // n_x, columns)
    act = exchange(jnp.broadcast_to(act, (n_x,) + act.shape[1:]), "x")
    own = act.reshape(half_rows, columns)
    other = lax.ppermute(own, "core", swap)
    own = near(own)
    held = call(
        own_kernel,
        [vmem] * 4,
        vmem,
        near_out((owners // n_core,) + block[1:]),
        (own, *weights),
        LIMIT,
    )
    grad = jax.ShapeDtypeStruct((1, local_width, grp_width), LOW)
    buf = pltpu.VMEM((1, local_width, grp_width), LOW)
    back, grad_gate, grad_up, grad_down = call(
        tail_kernel,
        [smem] + [vmem] * 7,
        (vmem, hbm, hbm, hbm),
        (near_out(block), grad, grad, grad),
        (half, own, near(other), got, held, *weights),
        TAIL_LIMIT,
        [buf, buf, buf, pltpu.SemaphoreType.DMA((3,))],
    )
    back = exchange(back, ("z_lo", "y"))
    flat = jax.ShapeDtypeStruct((tok_count, local_width), LOW)
    mixed, grad_tokens = call(
        final_kernel,
        [smem, smem, vmem],
        (vmem, vmem),
        (flat, flat),
        (routes_t, weights_t, near(back)),
        LIMIT,
    )
    return mixed, grad_tokens, grad_gate, grad_up, jnp.swapaxes(grad_down, 1, 2)


def solution(mesh):
    n_fsdp, n_expert = mesh.shape["fsdp"], mesh.shape["expert"]
    n_x = 4 if n_fsdp >= 32 else 2
    split = (n_x, n_fsdp // (2 * n_x), 2, EXPERTS, n_expert // EXPERTS)
    fine = Mesh(mesh.devices.reshape(split), ("x", "z_hi", "core", "z_lo", "y"))
    fsdp, expert = ("x", "z_hi", "core"), ("z_lo", "y")
    in_specs = (
        P(expert, fsdp),
        P(expert, fsdp),
        P(expert, None),
        P(expert, None),
        P(expert),
        P(),
        P(expert, fsdp, None),
        P(expert, fsdp, None),
        P(expert, None, fsdp),
    )
    out_specs = (
        P(expert, fsdp),
        P(expert, fsdp),
        P(expert, fsdp, None),
        P(expert, fsdp, None),
        P(expert, None, fsdp),
    )
    return jax.shard_map(
        per_device, mesh=fine, in_specs=in_specs, out_specs=out_specs, check_vma=False
    )
```

```python
import jax
import jax.numpy as jnp
from jax import lax
from jax.experimental import pallas as pl
from jax.experimental.pallas import tpu as pltpu
from jax.sharding import Mesh, PartitionSpec as P

EXPERTS = 4
TOP = 2
LIMIT = 8 * 2**20
TAIL_LIMIT = 16 * 2**20
INTERPRET = False
F32 = jnp.float32
LOW = jnp.bfloat16
NN = (((1,), (0,)), ((), ()))
NT = (((1,), (1,)), ((), ()))
TN = (((0,), (0,)), ((), ()))


def mm(a, b, dims):
    return lax.dot_general(a, b, dims, preferred_element_type=F32)


def column(values):
    spots = lax.broadcasted_iota(jnp.int32, (len(values), 1), 0)
    out = jnp.zeros((len(values), 1), F32)
    for t, value in enumerate(values):
        out = jnp.where(spots == t, value, out)
    return out


def expert_column(routes_ref, values, expert, count):
    picked = []
    for t in range(count):
        total = F32(0.0)
        for k in range(TOP):
            total = total + jnp.where(routes_ref[k, t] == expert, values(k, t), F32(0.0))
        picked.append(total)
    return column(picked)


def send_kernel(routes_ref, weights_ref, domains_ref, loss_ref, tok_ref, cot_ref, out_ref):
    count = tok_ref.shape[0]
    groups = out_ref.shape[0] // EXPERTS
    scale = column([loss_ref[domains_ref[t]] for t in range(count)])
    scaled = (cot_ref[...].astype(F32) * scale).astype(LOW).astype(F32)
    tok = tok_ref[...].astype(F32)
    for expert in range(EXPERTS):
        weight = expert_column(routes_ref, lambda k, t: weights_ref[k, t], expert, count)
        named = expert_column(routes_ref, lambda k, t: F32(1.0), expert, count)
        x_part = jnp.where(named > 0.0, tok, F32(0.0))
        g_part = weight * scaled
        both = jnp.concatenate([x_part, g_part], axis=1).astype(LOW)
        for group in range(groups):
            out_ref[expert * groups + group] = both


def final_kernel(routes_ref, weights_ref, back_ref, mixed_ref, grad_ref):
    count, width = mixed_ref.shape
    groups = back_ref.shape[0] // EXPERTS
    mixed, grad = None, None
    for expert in range(EXPERTS):
        weight = expert_column(routes_ref, lambda k, t: weights_ref[k, t], expert, count)
        total = back_ref[expert * groups].astype(F32)
        for group in range(1, groups):
            total = total + back_ref[expert * groups + group].astype(F32)
        out = weight * total
        mixed = out if mixed is None else mixed + out
        grad = total if grad is None else grad + total
    mixed_ref[...] = mixed[:, :width].astype(LOW)
    grad_ref[...] = grad[:, width:].astype(LOW)


def rows_of(ref, half):
    blocks, count, width = ref.shape
    blocks = blocks // 2
    return ref[pl.ds(half * blocks, blocks)].reshape(blocks * count, width)


def partial_kernel(half_ref, got_ref, wg_ref, wu_ref, wd_ref, out_ref, bufs, sems):
    width = bufs.shape[2]
    half = half_ref[0]
    copies = []
    for i, weight_ref in enumerate((wg_ref, wu_ref, wd_ref)):
        copy = pltpu.make_async_copy(weight_ref.at[0], bufs.at[i], sems.at[i])
        copy.start()
        copies.append(copy)
    both = rows_of(got_ref, half)
    depth = bufs.shape[1]
    for i, copy in enumerate(copies):
        rows = both[:, depth:] if i == 2 else both[:, :depth]
        copy.wait()
        out_ref[:, i * width : (i + 1) * width] = mm(rows, bufs[i], NN).astype(LOW)


def middle_kernel(parts_ref, out_ref):
    copies, _, columns = parts_ref.shape
    width = columns // 3
    total = parts_ref[0].astype(F32)
    for i in range(1, copies):
        total = total + parts_ref[i].astype(F32)
    gate = total[:, :width]
    up = total[:, width : 2 * width]
    hidden_grad = total[:, 2 * width :]
    sigma = jax.nn.sigmoid(gate)
    hidden = (gate * sigma * up).astype(LOW)
    gate_grad = (hidden_grad * up * sigma * (1.0 + gate * (1.0 - sigma))).astype(LOW)
    up_grad = (hidden_grad * gate * sigma).astype(LOW)
    for i in range(copies):
        out_ref[i, :, :width] = hidden
        out_ref[i, :, width : 2 * width] = gate_grad
        out_ref[i, :, 2 * width :] = up_grad


def row_products(act_ref, wg_ref, wu_ref, wd_ref):
    width = wg_ref.shape[2]
    out = mm(act_ref[:, :width], wd_ref[0], NT)
    inner = mm(act_ref[:, width : 2 * width], wg_ref[0], NT)
    inner = inner + mm(act_ref[:, 2 * width :], wu_ref[0], NT)
    return jnp.concatenate([out, inner], axis=1).astype(LOW)


def own_kernel(act_ref, wg_ref, wu_ref, wd_ref, back_ref):
    back_ref[...] = row_products(act_ref, wg_ref, wu_ref, wd_ref).reshape(back_ref.shape)


def tail_kernel(
    half_ref,
    own_ref,
    other_ref,
    got_ref,
    held_ref,
    wg_ref,
    wu_ref,
    wd_ref,
    back_ref,
    gg_ref,
    gu_ref,
    gd_ref,
    gg_buf,
    gu_buf,
    gd_buf,
    sems,
):
    width = wg_ref.shape[2]
    blocks = held_ref.shape[0]
    half = half_ref[0]
    act = jnp.concatenate([own_ref[...], other_ref[...]], axis=0)
    both = jnp.concatenate([rows_of(got_ref, half), rows_of(got_ref, 1 - half)], axis=0)
    depth = both.shape[1] // 2
    copies = []
    for i, (buf, dst) in enumerate(((gd_buf, gd_ref), (gg_buf, gg_ref), (gu_buf, gu_ref))):
        rows = both[:, :depth] if i else both[:, depth:]
        buf[0] = mm(rows, act[:, i * width : (i + 1) * width], TN).astype(LOW)
        copy = pltpu.make_async_copy(buf, dst, sems.at[i])
        copy.start()
        copies.append(copy)
    rows = row_products(other_ref, wg_ref, wu_ref, wd_ref)
    back_ref[pl.ds(half * blocks, blocks)] = held_ref[...]
    back_ref[pl.ds((1 - half) * blocks, blocks)] = rows.reshape(held_ref.shape)
    for copy in copies:
        copy.wait()


def near(value):
    return value if INTERPRET else pltpu.with_memory_space_constraint(value, pltpu.VMEM)


def far(value):
    return value if INTERPRET else pltpu.with_memory_space_constraint(value, pltpu.HBM)


def near_out(shape):
    return jax.ShapeDtypeStruct(shape, LOW) if INTERPRET else pltpu.VMEM(shape, LOW)


def call(kernel, in_specs, out_specs, shapes, args, limit, scratch=()):
    return pl.pallas_call(
        kernel,
        out_shape=shapes,
        in_specs=in_specs,
        out_specs=out_specs,
        scratch_shapes=scratch,
        compiler_params=pltpu.CompilerParams(vmem_limit_bytes=limit),
        interpret=INTERPRET,
    )(*args)


def exchange(value, axis):
    return lax.all_to_all(value, axis, split_axis=0, concat_axis=0, tiled=True)


def per_device(
    tokens, cotangent, routes, route_weights, domains, loss_weights, w_gate, w_up, w_down
):
    tok_count, local_width = tokens.shape
    n_x, n_z, n_core = lax.axis_size("x"), lax.axis_size("z_hi"), lax.axis_size("core")
    owners = EXPERTS * lax.axis_size("y")
    grp_width = w_gate.shape[2]
    columns = 3 * grp_width
    half_rows = owners * tok_count // n_core
    routes_t = routes.T
    weights_t = route_weights.T
    half = lax.axis_index("core").reshape(1).astype(jnp.int32)
    swap = [(0, 1), (1, 0)]
    plain_weights = (w_gate, w_up, jnp.swapaxes(w_down, 1, 2))
    far_weights = [far(w) for w in plain_weights]
    weights = [near(w) for w in plain_weights]

    smem = pl.BlockSpec(memory_space=pltpu.SMEM)
    vmem = pl.BlockSpec(memory_space=pltpu.VMEM)
    hbm = pl.BlockSpec(memory_space=pl.ANY)
    block = (owners, tok_count, 2 * local_width)
    send = call(
        send_kernel,
        [smem] * 4 + [vmem] * 2,
        vmem,
        near_out(block),
        (routes_t, weights_t, domains, loss_weights, tokens, cotangent),
        None,
    )
    send, half, rest = lax.optimization_barrier((send, half, 1 - half))
    got = near(exchange(send, ("z_lo", "y")))

    def partial(which):
        return call(
            partial_kernel,
            [smem, vmem] + [pl.BlockSpec(memory_space=pl.ANY if INTERPRET else pltpu.HBM)] * 3,
            vmem,
            near_out((half_rows, columns)),
            (which, got, *far_weights),
            LIMIT,
            [
                pltpu.VMEM((3, local_width, grp_width), LOW),
                pltpu.SemaphoreType.DMA((3,)),
            ],
        )

    arrived = lax.ppermute(partial(rest), "core", swap)
    sums = (partial(half).astype(F32) + arrived.astype(F32)).astype(LOW)
    parts = exchange(sums.reshape(n_x, half_rows // n_x, columns), "x")
    sums = jnp.sum(parts.astype(F32), axis=0).astype(LOW)
    parts = exchange(sums.reshape(n_z, sums.shape[0] // n_z, columns), "z_hi")
    copies = call(middle_kernel, [vmem], vmem, near_out(parts.shape), (near(parts),), LIMIT)
    act = exchange(copies, "z_hi").reshape(1, half_rows // n_x, columns)
    act = exchange(jnp.broadcast_to(act, (n_x,) + act.shape[1:]), "x")
    own = act.reshape(half_rows, columns)
    other = lax.ppermute(own, "core", swap)
    own = near(own)
    held = call(
        own_kernel,
        [vmem] * 4,
        vmem,
        near_out((owners // n_core,) + block[1:]),
        (own, *weights),
        LIMIT,
    )
    grad = jax.ShapeDtypeStruct((1, local_width, grp_width), LOW)
    buf = pltpu.VMEM((1, local_width, grp_width), LOW)
    back, grad_gate, grad_up, grad_down = call(
        tail_kernel,
        [smem] + [vmem] * 7,
        (vmem, hbm, hbm, hbm),
        (near_out(block), grad, grad, grad),
        (half, own, near(other), got, held, *weights),
        TAIL_LIMIT,
        [buf, buf, buf, pltpu.SemaphoreType.DMA((3,))],
    )
    back = exchange(back, ("z_lo", "y"))
    flat = jax.ShapeDtypeStruct((tok_count, local_width), LOW)
    mixed, grad_tokens = call(
        final_kernel,
        [smem, smem, vmem],
        (vmem, vmem),
        (flat, flat),
        (routes_t, weights_t, near(back)),
        LIMIT,
    )
    return mixed, grad_tokens, grad_gate, grad_up, jnp.swapaxes(grad_down, 1, 2)


def solution(mesh):
    n_fsdp, n_expert = mesh.shape["fsdp"], mesh.shape["expert"]
    n_x = 4 if n_fsdp >= 32 else 2
    split = (n_x, n_fsdp // (2 * n_x), 2, EXPERTS, n_expert // EXPERTS)
    fine = Mesh(mesh.devices.reshape(split), ("x", "z_hi", "core", "z_lo", "y"))
    fsdp, expert = ("x", "z_hi", "core"), ("z_lo", "y")
    in_specs = (
        P(expert, fsdp),
        P(expert, fsdp),
        P(expert, None),
        P(expert, None),
        P(expert),
        P(),
        P(expert, fsdp, None),
        P(expert, fsdp, None),
        P(expert, None, fsdp),
    )
    out_specs = (
        P(expert, fsdp),
        P(expert, fsdp),
        P(expert, fsdp, None),
        P(expert, fsdp, None),
        P(expert, None, fsdp),
    )
    return jax.shard_map(
        per_device, mesh=fine, in_specs=in_specs, out_specs=out_specs, check_vma=False
    )
```

```python
import jax
import jax.numpy as jnp
from jax import lax
from jax.experimental import pallas as pl
from jax.experimental.pallas import tpu as pltpu
from jax.sharding import Mesh, PartitionSpec as P

EXPERTS = 4
TOP = 2
LIMIT = 8 * 2**20
TAIL_LIMIT = 16 * 2**20
INTERPRET = False
F32 = jnp.float32
LOW = jnp.bfloat16
NN = (((1,), (0,)), ((), ()))
NT = (((1,), (1,)), ((), ()))
TN = (((0,), (0,)), ((), ()))


def mm(a, b, dims):
    return lax.dot_general(a, b, dims, preferred_element_type=F32)


def column(values):
    spots = lax.broadcasted_iota(jnp.int32, (len(values), 1), 0)
    out = jnp.zeros((len(values), 1), F32)
    for t, value in enumerate(values):
        out = jnp.where(spots == t, value, out)
    return out


def expert_column(routes_ref, values, expert, count):
    picked = []
    for t in range(count):
        total = F32(0.0)
        for k in range(TOP):
            total = total + jnp.where(routes_ref[k, t] == expert, values(k, t), F32(0.0))
        picked.append(total)
    return column(picked)


def send_kernel(routes_ref, weights_ref, domains_ref, loss_ref, tok_ref, cot_ref, out_ref):
    count = tok_ref.shape[0]
    groups = out_ref.shape[0] // EXPERTS
    scale = column([loss_ref[domains_ref[t]] for t in range(count)])
    scaled = (cot_ref[...].astype(F32) * scale).astype(LOW).astype(F32)
    tok = tok_ref[...].astype(F32)
    for expert in range(EXPERTS):
        weight = expert_column(routes_ref, lambda k, t: weights_ref[k, t], expert, count)
        named = expert_column(routes_ref, lambda k, t: F32(1.0), expert, count)
        x_part = jnp.where(named > 0.0, tok, F32(0.0))
        g_part = weight * scaled
        both = jnp.concatenate([x_part, g_part], axis=1).astype(LOW)
        for group in range(groups):
            out_ref[expert * groups + group] = both


def final_kernel(routes_ref, weights_ref, back_ref, mixed_ref, grad_ref):
    count, width = mixed_ref.shape
    groups = back_ref.shape[0] // EXPERTS
    mixed, grad = None, None
    for expert in range(EXPERTS):
        weight = expert_column(routes_ref, lambda k, t: weights_ref[k, t], expert, count)
        total = back_ref[expert * groups].astype(F32)
        for group in range(1, groups):
            total = total + back_ref[expert * groups + group].astype(F32)
        out = weight * total
        mixed = out if mixed is None else mixed + out
        grad = total if grad is None else grad + total
    mixed_ref[...] = mixed[:, :width].astype(LOW)
    grad_ref[...] = grad[:, width:].astype(LOW)


def rows_of(ref, half):
    blocks, count, width = ref.shape
    blocks = blocks // 2
    return ref[pl.ds(half * blocks, blocks)].reshape(blocks * count, width)


def partial_kernel(half_ref, got_ref, wg_ref, wu_ref, wd_ref, out_ref, bufs, sems):
    width = bufs.shape[2]
    half = half_ref[0]
    copies = []
    for i, weight_ref in enumerate((wg_ref, wu_ref, wd_ref)):
        copy = pltpu.make_async_copy(weight_ref.at[0], bufs.at[i], sems.at[i])
        copy.start()
        copies.append(copy)
    both = rows_of(got_ref, half)
    depth = bufs.shape[1]
    for i, copy in enumerate(copies):
        rows = both[:, depth:] if i == 2 else both[:, :depth]
        copy.wait()
        out_ref[:, i * width : (i + 1) * width] = mm(rows, bufs[i], NN).astype(LOW)


def middle_kernel(parts_ref, out_ref):
    copies, _, columns = parts_ref.shape
    width = columns // 3
    total = parts_ref[0].astype(F32)
    for i in range(1, copies):
        total = total + parts_ref[i].astype(F32)
    gate = total[:, :width]
    up = total[:, width : 2 * width]
    hidden_grad = total[:, 2 * width :]
    sigma = jax.nn.sigmoid(gate)
    hidden = (gate * sigma * up).astype(LOW)
    gate_grad = (hidden_grad * up * sigma * (1.0 + gate * (1.0 - sigma))).astype(LOW)
    up_grad = (hidden_grad * gate * sigma).astype(LOW)
    out_ref[:, :width] = hidden
    out_ref[:, width : 2 * width] = gate_grad
    out_ref[:, 2 * width :] = up_grad


def row_products(act_ref, wg_ref, wu_ref, wd_ref):
    width = wg_ref.shape[2]
    out = mm(act_ref[:, :width], wd_ref[0], NT)
    inner = mm(act_ref[:, width : 2 * width], wg_ref[0], NT)
    inner = inner + mm(act_ref[:, 2 * width :], wu_ref[0], NT)
    return jnp.concatenate([out, inner], axis=1).astype(LOW)


def own_kernel(act_ref, wg_ref, wu_ref, wd_ref, back_ref):
    back_ref[...] = row_products(act_ref, wg_ref, wu_ref, wd_ref).reshape(back_ref.shape)


def tail_kernel(
    half_ref,
    own_ref,
    other_ref,
    got_ref,
    held_ref,
    wg_ref,
    wu_ref,
    wd_ref,
    back_ref,
    gg_ref,
    gu_ref,
    gd_ref,
    gg_buf,
    gu_buf,
    gd_buf,
    sems,
):
    width = wg_ref.shape[2]
    blocks = held_ref.shape[0]
    half = half_ref[0]
    act = jnp.concatenate([own_ref[...], other_ref[...]], axis=0)
    both = jnp.concatenate([rows_of(got_ref, half), rows_of(got_ref, 1 - half)], axis=0)
    depth = both.shape[1] // 2
    copies = []
    for i, (buf, dst) in enumerate(((gd_buf, gd_ref), (gg_buf, gg_ref), (gu_buf, gu_ref))):
        rows = both[:, :depth] if i else both[:, depth:]
        buf[0] = mm(rows, act[:, i * width : (i + 1) * width], TN).astype(LOW)
        copy = pltpu.make_async_copy(buf, dst, sems.at[i])
        copy.start()
        copies.append(copy)
    rows = row_products(other_ref, wg_ref, wu_ref, wd_ref)
    back_ref[pl.ds(half * blocks, blocks)] = held_ref[...]
    back_ref[pl.ds((1 - half) * blocks, blocks)] = rows.reshape(held_ref.shape)
    for copy in copies:
        copy.wait()


def near(value):
    return value if INTERPRET else pltpu.with_memory_space_constraint(value, pltpu.VMEM)


def far(value):
    return value if INTERPRET else pltpu.with_memory_space_constraint(value, pltpu.HBM)


def near_out(shape):
    return jax.ShapeDtypeStruct(shape, LOW) if INTERPRET else pltpu.VMEM(shape, LOW)


def call(kernel, in_specs, out_specs, shapes, args, limit, scratch=()):
    return pl.pallas_call(
        kernel,
        out_shape=shapes,
        in_specs=in_specs,
        out_specs=out_specs,
        scratch_shapes=scratch,
        compiler_params=pltpu.CompilerParams(vmem_limit_bytes=limit),
        interpret=INTERPRET,
    )(*args)


def exchange(value, axis):
    return lax.all_to_all(value, axis, split_axis=0, concat_axis=0, tiled=True)


def per_device(
    tokens, cotangent, routes, route_weights, domains, loss_weights, w_gate, w_up, w_down
):
    tok_count, local_width = tokens.shape
    n_x, n_z, n_core = lax.axis_size("x"), lax.axis_size("z_hi"), lax.axis_size("core")
    owners = EXPERTS * lax.axis_size("y")
    grp_width = w_gate.shape[2]
    columns = 3 * grp_width
    half_rows = owners * tok_count // n_core
    routes_t = routes.T
    weights_t = route_weights.T
    half = lax.axis_index("core").reshape(1).astype(jnp.int32)
    swap = [(0, 1), (1, 0)]
    plain_weights = (w_gate, w_up, jnp.swapaxes(w_down, 1, 2))
    far_weights = [far(w) for w in plain_weights]
    weights = [near(w) for w in plain_weights]

    smem = pl.BlockSpec(memory_space=pltpu.SMEM)
    vmem = pl.BlockSpec(memory_space=pltpu.VMEM)
    hbm = pl.BlockSpec(memory_space=pl.ANY)
    block = (owners, tok_count, 2 * local_width)
    send = call(
        send_kernel,
        [smem] * 4 + [vmem] * 2,
        vmem,
        near_out(block),
        (routes_t, weights_t, domains, loss_weights, tokens, cotangent),
        None,
    )
    send, half, rest = lax.optimization_barrier((send, half, 1 - half))
    got = near(exchange(send, ("z_lo", "y")))

    def partial(which):
        return call(
            partial_kernel,
            [smem, vmem] + [pl.BlockSpec(memory_space=pl.ANY if INTERPRET else pltpu.HBM)] * 3,
            vmem,
            near_out((half_rows, columns)),
            (which, got, *far_weights),
            LIMIT,
            [
                pltpu.VMEM((3, local_width, grp_width), LOW),
                pltpu.SemaphoreType.DMA((3,)),
            ],
        )

    arrived = lax.ppermute(partial(rest), "core", swap)
    sums = (partial(half).astype(F32) + arrived.astype(F32)).astype(LOW)
    parts = exchange(sums.reshape(n_x, half_rows // n_x, columns), "x")
    sums = jnp.sum(parts.astype(F32), axis=0).astype(LOW)
    parts = exchange(sums.reshape(n_z, sums.shape[0] // n_z, columns), "z_hi")
    act = call(middle_kernel, [vmem], vmem, near_out(parts.shape[1:]), (near(parts),), LIMIT)
    act = lax.all_gather(act, "z_hi", axis=0, tiled=True)[None]
    act = exchange(jnp.broadcast_to(act, (n_x,) + act.shape[1:]), "x")
    own = act.reshape(half_rows, columns)
    other = lax.ppermute(own, "core", swap)
    own = near(own)
    held = call(
        own_kernel,
        [vmem] * 4,
        vmem,
        near_out((owners // n_core,) + block[1:]),
        (own, *weights),
        LIMIT,
    )
    grad = jax.ShapeDtypeStruct((1, local_width, grp_width), LOW)
    buf = pltpu.VMEM((1, local_width, grp_width), LOW)
    back, grad_gate, grad_up, grad_down = call(
        tail_kernel,
        [smem] + [vmem] * 7,
        (vmem, hbm, hbm, hbm),
        (near_out(block), grad, grad, grad),
        (half, own, near(other), got, held, *weights),
        TAIL_LIMIT,
        [buf, buf, buf, pltpu.SemaphoreType.DMA((3,))],
    )
    back = exchange(back, ("z_lo", "y"))
    flat = jax.ShapeDtypeStruct((tok_count, local_width), LOW)
    mixed, grad_tokens = call(
        final_kernel,
        [smem, smem, vmem],
        (vmem, vmem),
        (flat, flat),
        (routes_t, weights_t, near(back)),
        LIMIT,
    )
    return mixed, grad_tokens, grad_gate, grad_up, jnp.swapaxes(grad_down, 1, 2)


def solution(mesh):
    n_fsdp, n_expert = mesh.shape["fsdp"], mesh.shape["expert"]
    n_x = 4 if n_fsdp >= 32 else 2
    split = (n_x, n_fsdp // (2 * n_x), 2, EXPERTS, n_expert // EXPERTS)
    fine = Mesh(mesh.devices.reshape(split), ("x", "z_hi", "core", "z_lo", "y"))
    fsdp, expert = ("x", "z_hi", "core"), ("z_lo", "y")
    in_specs = (
        P(expert, fsdp),
        P(expert, fsdp),
        P(expert, None),
        P(expert, None),
        P(expert),
        P(),
        P(expert, fsdp, None),
        P(expert, fsdp, None),
        P(expert, None, fsdp),
    )
    out_specs = (
        P(expert, fsdp),
        P(expert, fsdp),
        P(expert, fsdp, None),
        P(expert, fsdp, None),
        P(expert, None, fsdp),
    )
    return jax.shard_map(
        per_device, mesh=fine, in_specs=in_specs, out_specs=out_specs, check_vma=False
    )
```
